32 devices in a mesh: row: 4 (over y, x), col: 4 (over z), depth: 2 (over core).
Axes of the slice: x: 2, y: 2, z: 4, core: 2. Of those that a mesh axis runs over, the one named last changes fastest.
Arguments:
- p_blocks: float32 [40, 4, 6, 128, 128], P('row', 'col', 'depth'), may hold values from -0.125 to 0.125
- s_blocks: float32 [40, 4, 6, 128, 128], P('row', 'col'), may hold values from -6 to 6
- p_pattern: int32 [40, 4, 6], P('row'), may hold values from -1 to 39, as said below
- s_pattern: int32 [40, 4, 6], P(None, 'col'), may hold values from -1 to 39, as said below
Outputs:
- product: float32 [40, 4, 6, 128, 128], P('row', 'col', 'depth')
The draws below stay inside these ranges and needn't reach their ends.
Inputs may be any that keep to these rules, and one draw needn't show every extreme that they name: `p_pattern`: in each row and group of slots the filled slots come first. Every block column belongs to one grid column, the same in both patterns, and appears only in that group of slots; the columns of a block row are distinct and lie within cyclic distance 10 of the row, modulo 40. Some block row fills all 6 slots of some group. `s_pattern`: as for p_pattern, with the same grid column for each block column.
All inputs are finite; a program needn't handle non-finite values.
Results may differ from the reference program's by a relative error of at most 0.0003.
Values sent between devices are 32-bit elements; how exact they have to be, the bound alone decides.
No kernel may reach another device: no remote copies, remote signals or barrier semaphores. Data moves between devices by JAX's collectives and lax.ppermute only.
A program may use at most 128 MiB of HBM per device.

```python
import jax
import jax.numpy as jnp
from jax import lax

BS = 128
W = 10
NB = 40
KT = 6
N_COL = 4


def owner_table(key):
    run_count = NB // N_COL
    key_list = jax.random.split(jax.random.fold_in(key, 7), run_count)
    shuffles = jax.vmap(lambda sub_key: jax.random.permutation(sub_key, N_COL))(key_list)
    return shuffles.reshape(NB).astype(jnp.int32)


def pattern(key, stream_id):
    owners = owner_table(key)
    offsets = jnp.arange(2 * W + 1, dtype=jnp.int32) - W
    row_ids = jnp.arange(NB, dtype=jnp.int32)
    column_ids = (row_ids[:, None] + offsets[None, :]) % NB
    coin_toss = jax.random.randint(jax.random.fold_in(key, stream_id), (NB, 2 * W + 1), 0, 4)
    full_rows = jax.random.randint(jax.random.fold_in(key, stream_id + 100), (NB,), 0, 4)
    whole_row = (full_rows == 0) | (row_ids == 0)
    kept_mask = (coin_toss != 0) | whole_row[:, None] | (offsets[None, :] == 0)
    group_ids = owners[column_ids]
    member = kept_mask[:, None, :] & (group_ids[:, None, :] == jnp.arange(N_COL, dtype=jnp.int32)[None, :, None])
    position = jnp.cumsum(member.astype(jnp.int32), axis=2) - 1
    slot_hit = member[..., None] & (position[..., None] == jnp.arange(KT, dtype=jnp.int32)[None, None, None, :])
    filled = jnp.any(slot_hit, axis=2)
    picked = jnp.sum(jnp.where(slot_hit, column_ids[:, None, :, None], 0), axis=2)
    return jnp.where(filled, picked, -1).astype(jnp.int32)


def draw_p_pattern(key, part):
    return pattern(key, 1)


def draw_s_pattern(key, part):
    return pattern(key, 2)


def level_of(stream_key, dims, cuts, low, top_value):
    def one(axis_at, parts):
        steps = jax.random.uniform(jax.random.fold_in(jax.random.fold_in(stream_key, 6), axis_at), (parts,), jnp.float32, low / len(cuts), top_value / len(cuts))
        return jnp.repeat(jnp.exp(steps), dims[axis_at] // parts).reshape((-1,) + (1,) * (len(dims) - axis_at - 1))

    level = one(*cuts[0])
    for cut in cuts[1:]:
        level = level * one(*cut)
    return level


def bell_draw(rng, shape, spread, limit, cuts=(), kind=jnp.bfloat16):
    result = spread * jax.random.normal(rng, shape, jnp.float32)
    if cuts:
        result = result * level_of(rng, shape, cuts, -0.22, 0.18)
    return jnp.clip(result, -limit, limit).astype(kind)


def setup_inputs(seed: int = 0) -> dict:
    seeds = jax.random.split(jax.random.key(seed), 5)
    return {
        "p_blocks": bell_draw(seeds[0], (NB, N_COL, KT, BS, BS), (BS * 2 * W) ** -0.5, 0.125, ((0, 4), (1, 4), (2, 2)), jnp.float32),
        "s_blocks": bell_draw(seeds[1], (NB, N_COL, KT, BS, BS), 1.0, 6.0, ((0, 4), (1, 4)), jnp.float32),
        "p_pattern": draw_p_pattern(jax.random.fold_in(seeds[4], 71), 0),
        "s_pattern": draw_s_pattern(jax.random.fold_in(seeds[4], 71), 0),
    }


def reference(p_blocks, s_blocks, p_pattern, s_pattern):
    s_flat = s_blocks.reshape(NB * N_COL * KT, BS, BS)
    slot_ids = jnp.arange(KT, dtype=jnp.int32)
    group_ids = jnp.arange(N_COL, dtype=jnp.int32)

    def one_row(inputs):
        p_row, col_row = inputs
        inner = col_row.reshape(N_COL * KT)
        safe_cols = jnp.maximum(inner, 0)
        s_rows = s_pattern[safe_cols]
        matches = (s_rows[:, :, None, :] == col_row[None, :, :, None]) & (col_row >= 0)[None, :, :, None] & (inner >= 0)[:, None, None, None]
        picked = jnp.sum(jnp.where(matches, slot_ids, 0), axis=3).astype(jnp.int32)
        found = jnp.any(matches, axis=3)
        index = ((safe_cols[:, None, None] * N_COL + group_ids[None, :, None]) * KT + picked).astype(jnp.int32)
        chosen = jnp.where(found[..., None, None], s_flat[index], jnp.zeros((), s_flat.dtype))
        left_blocks = p_row.reshape(N_COL * KT, BS, BS)
        return jnp.einsum('amn,agcnp->gcmp', left_blocks, chosen, precision=lax.Precision.HIGHEST)

    return lax.map(one_row, (p_blocks, p_pattern))
```

```python
import functools

import jax
import jax.numpy as jnp
from jax import lax
from jax.experimental import pallas as pl
from jax.experimental.pallas import tpu as pltpu
from jax.sharding import PartitionSpec as P


def split_store(value, ref, index):
    width = value.shape[-1]
    head = value.astype(jnp.bfloat16)
    tail = (value - head.astype(jnp.float32)).astype(jnp.bfloat16)
    ref[index, :, 0:width] = head
    ref[index, :, width : 2 * width] = tail


def prepare_own(s_own, total_groups):
    rows, slots, size, _ = s_own.shape

    def body(s_ref, out_ref):
        step = pl.program_id(0)

        @pl.when(step < rows)
        def _():
            for slot in range(slots):
                split_store(s_ref[0, slot], out_ref, slot)

        @pl.when(step == rows)
        def _():
            out_ref[...] = jnp.zeros_like(out_ref)

    return pl.pallas_call(
        body,
        grid=(rows + 1,),
        in_specs=[
            pl.BlockSpec((1, slots, size, size), lambda g: (jnp.minimum(g, rows - 1), 0, 0, 0))
        ],
        out_specs=pl.BlockSpec(
            (slots, size, 2 * size), lambda g: (jnp.where(g < rows, g, total_groups - 1), 0, 0)
        ),
        out_shape=jax.ShapeDtypeStruct((total_groups * slots, size, 2 * size), jnp.bfloat16),
        name="prepare_own",
    )(s_own)


def prepare_halo(buffer, mine, other, first_group):
    rows, slots, size, _ = mine.shape

    def body(mine_ref, other_ref, buffer_ref, out_ref):
        step = pl.program_id(0)

        @pl.when(step < rows)
        def _():
            for slot in range(slots):
                split_store(mine_ref[0, slot], out_ref, slot)

        @pl.when(step >= rows)
        def _():
            for slot in range(slots):
                split_store(other_ref[0, slot], out_ref, slot)

    block = (1, slots, size, size)
    return pl.pallas_call(
        body,
        grid=(2 * rows,),
        in_specs=[
            pl.BlockSpec(block, lambda g: (jnp.minimum(g, rows - 1), 0, 0, 0)),
            pl.BlockSpec(block, lambda g: (jnp.maximum(g - rows, 0), 0, 0, 0)),
            pl.BlockSpec(memory_space=pl.ANY),
        ],
        out_specs=pl.BlockSpec((slots, size, 2 * size), lambda g: (g + first_group, 0, 0)),
        out_shape=jax.ShapeDtypeStruct(buffer.shape, buffer.dtype),
        input_output_aliases={2: 0},
        name="prepare_halo",
    )(mine, other, buffer)


def multiply(table, groups, valid, pieces, s_split, total):
    rows, half, size, _ = pieces[0][0].shape
    count = len(pieces)
    inner = 2 * half

    def body(table_ref, groups_ref, valid_ref, *refs):
        piece_refs = refs[: 2 * count]
        s_ref = refs[2 * count]
        out_ref, left_ref = refs[-2], refs[-1]
        row = pl.program_id(0)
        if total is None:
            out_ref[...] = jnp.zeros_like(out_ref)
        else:
            out_ref[...] = refs[2 * count + 1][...]
        for piece in range(count):

            @pl.when(valid_ref[piece] == 1)
            def _():
                for part in range(2):
                    for slot in range(half):
                        value = piece_refs[2 * piece + part][0, slot]
                        head = value.astype(jnp.bfloat16)
                        tail = (value - head.astype(jnp.float32)).astype(jnp.bfloat16)
                        at = (part * half + slot) * size
                        left_ref[0:size, at : at + size] = head
                        left_ref[size : 2 * size, at : at + size] = tail
                base = (groups_ref[piece] * rows + row) * half * inner
                for target in range(half):
                    right = jnp.concatenate(
                        [s_ref[table_ref[base + target * inner + a]] for a in range(inner)], axis=0
                    )
                    got = jnp.dot(left_ref[...], right, preferred_element_type=jnp.float32)
                    low = got[0:size, size:] + got[size:, 0:size] + got[size:, size:]
                    out_ref[0, target] += got[0:size, 0:size] + low

    def piece_spec(piece):
        return pl.BlockSpec(
            (1, half, size, size),
            lambda i, table_ref, groups_ref, valid_ref: (i * valid_ref[piece], 0, 0, 0),
        )

    row_spec = pl.BlockSpec((1, half, size, size), lambda i, *_: (i, 0, 0, 0))
    in_specs = [piece_spec(n // 2) for n in range(2 * count)]
    in_specs.append(pl.BlockSpec(memory_space=pltpu.VMEM))
    operands = [part for piece in pieces for part in piece] + [s_split]
    aliases = {}
    if total is not None:
        in_specs.append(row_spec)
        operands.append(total)
        aliases = {3 + len(operands) - 1: 0}
    return pl.pallas_call(
        body,
        grid_spec=pltpu.PrefetchScalarGridSpec(
            num_scalar_prefetch=3,
            grid=(rows,),
            in_specs=in_specs,
            out_specs=row_spec,
            scratch_shapes=[pltpu.VMEM((2 * size, inner * size), jnp.bfloat16)],
        ),
        out_shape=jax.ShapeDtypeStruct((rows, half, size, size), jnp.float32),
        input_output_aliases=aliases,
        name="multiply",
    )(table, groups, valid, *operands)


def make_table(p_pattern, s_pattern, grid_col, layer, half, bases, zero_block):
    rows, groups, slots = p_pattern.shape
    mine = lax.dynamic_slice_in_dim(p_pattern, layer * half, half, 2)
    other = lax.dynamic_slice_in_dim(p_pattern, (1 - layer) * half, half, 2)
    inner = jnp.concatenate([mine, other], axis=2)
    targets = lax.dynamic_index_in_dim(mine, grid_col, 1, keepdims=False)
    total_rows = s_pattern.shape[0]
    ids = jnp.arange(total_rows, dtype=jnp.int32)
    hot = (inner.reshape(-1, 1) == ids[None, :]).astype(jnp.float32)
    lookup = jnp.concatenate([s_pattern[:, 0, :], bases[:, None]], axis=1).astype(jnp.float32)
    found = jnp.einsum("nk,kb->nb", hot, lookup, precision=lax.Precision.HIGHEST)
    found = found.astype(jnp.int32).reshape(rows, groups, slots, -1)
    s_rows, base = found[..., :-1], found[..., -1]
    match = (s_rows[:, :, None, :, :] == targets[:, None, :, None, None]) & (
        (targets >= 0)[:, None, :, None, None] & (inner >= 0)[:, :, None, :, None]
    )
    offset = jnp.arange(s_rows.shape[-1], dtype=jnp.int32)
    place = jnp.where(match, base[:, :, None, :, None] + offset - zero_block, 0)
    table = jnp.sum(place, axis=-1) + zero_block
    return jnp.transpose(table, (1, 0, 2, 3)).reshape(-1)


def per_device(p_blocks, s_blocks, p_pattern, s_pattern):
    rows, _, half, size, _ = p_blocks.shape
    slots = s_blocks.shape[2]
    n_row, n_col = lax.axis_size("row"), lax.axis_size("col")
    n_layer = lax.axis_size("depth")
    grid_row, grid_col = lax.axis_index("row"), lax.axis_index("col")
    layer = lax.axis_index("depth")
    row_half = rows // n_layer
    swap = [(0, 1), (1, 0)]

    def swap_where(keep):
        return [
            (z * n_layer + a, z * n_layer + b) for z in range(n_col) if keep(z) for a, b in swap
        ]

    p_mine = p_blocks[:, 0]
    steps = []
    up = down = p_mine
    for s in range(1, n_col):
        up = lax.ppermute(up, "col", [(i, i + 1) for i in range(s - 1, n_col - 1)])
        down = lax.ppermute(down, "col", [(i, i - 1) for i in range(1, n_col - s + 1)])
        steps.append((up, down))

    s_own = s_blocks[:, 0]
    s_half = lax.dynamic_slice_in_dim(s_own, layer * row_half, row_half, 0)
    if n_row == 4:
        near, far = grid_row ^ 1, grid_row ^ 3
        near_mine = lax.ppermute(s_half, "row", [(r, r ^ 1) for r in range(n_row)])
        far_mine = lax.ppermute(near_mine, "row", [(r, r ^ 2) for r in range(n_row)])
    else:
        near, far = (grid_row - 1) % n_row, (grid_row + 1) % n_row
        near_mine = lax.ppermute(s_half, "row", [(r, (r + 1) % n_row) for r in range(n_row)])
        far_mine = lax.ppermute(s_half, "row", [(r, (r - 1) % n_row) for r in range(n_row)])
    near_other = lax.ppermute(near_mine, "depth", swap)
    far_other = lax.ppermute(far_mine, "depth", swap)

    all_rows = jnp.arange(rows * n_row, dtype=jnp.int32)
    shard, local = all_rows // rows, all_rows % rows
    third = jnp.where(shard == near, 1, 2) * rows * slots
    halo = third + jnp.where(local // row_half == layer, 0, row_half * slots)
    bases = jnp.where(shard == grid_row, local * slots, halo + (local % row_half) * slots)
    total_groups = 3 * rows + 1
    zero_block = 3 * rows * slots
    table = make_table(p_pattern, s_pattern, grid_col, layer, half, bases, zero_block)

    s_split = prepare_own(s_own, total_groups)
    s_split = prepare_halo(s_split, near_mine, near_other, rows)
    s_split = prepare_halo(s_split, far_mine, far_other, 2 * rows)

    one = jnp.ones((), jnp.int32)
    p_other = lax.ppermute(p_mine, "depth", swap)
    pending = [(p_mine, p_other, grid_col, one)]
    result = None
    for s, (up, down) in enumerate(steps, 1):
        up_other = lax.ppermute(up, ("col", "depth"), swap_where(lambda z: z >= s))
        down_other = lax.ppermute(down, ("col", "depth"), swap_where(lambda z: z + s < n_col))
        pending.append((up, up_other, jnp.maximum(grid_col - s, 0), (grid_col >= s).astype(jnp.int32)))
        pending.append(
            (
                down,
                down_other,
                jnp.minimum(grid_col + s, n_col - 1),
                (grid_col + s < n_col).astype(jnp.int32),
            )
        )
        if s >= n_col - 2:
            groups = jnp.stack([item[2] for item in pending]).astype(jnp.int32)
            valid = jnp.stack([item[3] for item in pending])
            result = multiply(table, groups, valid, [item[:2] for item in pending], s_split, result)
            pending = []
    return result[:, None]


def solution(mesh):
    in_specs = (
        P("row", "col", "depth", None, None),
        P("row", "col", None, None, None),
        P("row", None, None),
        P(None, "col", None),
    )
    out_specs = P("row", "col", "depth", None, None)
    return jax.shard_map(
        per_device, mesh=mesh, in_specs=in_specs, out_specs=out_specs, check_vma=False
    )
```

```python
import jax
import jax.numpy as jnp
from jax import lax
from jax.experimental import pallas as pl
from jax.experimental.pallas import tpu as pltpu
from jax.sharding import PartitionSpec as P


CHUNKS = 2
VMEM_LIMIT = 24 << 20


def split_store(value, ref, index):
    width = value.shape[-1]
    head = value.astype(jnp.bfloat16)
    tail = (value - head.astype(jnp.float32)).astype(jnp.bfloat16)
    ref[index, :, 0:width] = head
    ref[index, :, width : 2 * width] = tail


def prepare_own(table, s_own, total_groups):
    rows, slots, size, _ = s_own.shape

    def body(table_ref, s_ref, out_ref):
        step = pl.program_id(0)

        @pl.when(step < rows)
        def _():
            for slot in range(slots):
                split_store(s_ref[0, slot], out_ref, slot)

        @pl.when(step == rows)
        def _():
            out_ref[...] = jnp.zeros_like(out_ref)

    return pl.pallas_call(
        body,
        grid_spec=pltpu.PrefetchScalarGridSpec(
            num_scalar_prefetch=1,
            grid=(rows + 1,),
            in_specs=[
                pl.BlockSpec(
                    (1, slots, size, size), lambda g, _: (jnp.minimum(g, rows - 1), 0, 0, 0)
                )
            ],
            out_specs=pl.BlockSpec(
                (slots, size, 2 * size),
                lambda g, _: (jnp.where(g < rows, g, total_groups - 1), 0, 0),
            ),
        ),
        out_shape=jax.ShapeDtypeStruct((total_groups * slots, size, 2 * size), jnp.bfloat16),
        compiler_params=pltpu.CompilerParams(vmem_limit_bytes=VMEM_LIMIT),
        name="prepare_own",
    )(table, s_own)


def prepare_halo(buffer, mine, other, first_group):
    rows, slots, size, _ = mine.shape

    def body(mine_ref, other_ref, buffer_ref, out_ref):
        step = pl.program_id(0)

        @pl.when(step < rows)
        def _():
            for slot in range(slots):
                split_store(mine_ref[0, slot], out_ref, slot)

        @pl.when(step >= rows)
        def _():
            for slot in range(slots):
                split_store(other_ref[0, slot], out_ref, slot)

    block = (1, slots, size, size)
    return pl.pallas_call(
        body,
        grid=(2 * rows,),
        in_specs=[
            pl.BlockSpec(block, lambda g: (jnp.minimum(g, rows - 1), 0, 0, 0)),
            pl.BlockSpec(block, lambda g: (jnp.maximum(g - rows, 0), 0, 0, 0)),
            pl.BlockSpec(memory_space=pl.ANY),
        ],
        out_specs=pl.BlockSpec((slots, size, 2 * size), lambda g: (g + first_group, 0, 0)),
        out_shape=jax.ShapeDtypeStruct(buffer.shape, buffer.dtype),
        input_output_aliases={2: 0},
        compiler_params=pltpu.CompilerParams(vmem_limit_bytes=VMEM_LIMIT),
        name="prepare_halo",
    )(mine, other, buffer)


def multiply(table, offset, pieces, s_split, total, all_rows, first_row, fresh):
    rows, half, size, _ = pieces[0][0].shape
    count = len(pieces)
    inner = 2 * half

    def body(table_ref, *refs):
        piece_refs = refs[: 2 * count]
        s_ref = refs[2 * count]
        out_ref, left_ref = refs[-2], refs[-1]
        row = pl.program_id(0) + first_row
        if fresh:
            out_ref[...] = jnp.zeros_like(out_ref)
        else:
            out_ref[...] = refs[2 * count + 1][...]
        for piece in range(count):

            @pl.when(table_ref[offset + 2 * piece + 1] == 1)
            def _():
                for part in range(2):
                    for slot in range(half):
                        value = piece_refs[2 * piece + part][0, slot]
                        head = value.astype(jnp.bfloat16)
                        tail = (value - head.astype(jnp.float32)).astype(jnp.bfloat16)
                        at = (part * half + slot) * size
                        left_ref[0:size, at : at + size] = head
                        left_ref[size : 2 * size, at : at + size] = tail
                base = (table_ref[offset + 2 * piece] * all_rows + row) * half * inner
                for target in range(half):
                    right = jnp.concatenate(
                        [s_ref[table_ref[base + target * inner + a]] for a in range(inner)], axis=0
                    )
                    got = jnp.dot(left_ref[...], right, preferred_element_type=jnp.float32)
                    low = got[0:size, size:] + got[size:, 0:size] + got[size:, size:]
                    out_ref[0, target] += got[0:size, 0:size] + low

    def piece_spec(piece):
        return pl.BlockSpec(
            (1, half, size, size),
            lambda i, table_ref: (i * table_ref[offset + 2 * piece + 1], 0, 0, 0),
        )

    row_spec = pl.BlockSpec((1, half, size, size), lambda i, *_: (i + first_row, 0, 0, 0))
    in_specs = [piece_spec(n // 2) for n in range(2 * count)]
    in_specs.append(pl.BlockSpec(memory_space=pltpu.VMEM))
    operands = [part for piece in pieces for part in piece] + [s_split]
    aliases = {}
    if total is not None:
        in_specs.append(pl.BlockSpec(memory_space=pl.ANY) if fresh else row_spec)
        operands.append(total)
        aliases = {1 + len(operands) - 1: 0}
    return pl.pallas_call(
        body,
        grid_spec=pltpu.PrefetchScalarGridSpec(
            num_scalar_prefetch=1,
            grid=(rows,),
            in_specs=in_specs,
            out_specs=row_spec,
            scratch_shapes=[pltpu.VMEM((2 * size, inner * size), jnp.bfloat16)],
        ),
        out_shape=jax.ShapeDtypeStruct((all_rows, half, size, size), jnp.float32),
        input_output_aliases=aliases,
        compiler_params=pltpu.CompilerParams(vmem_limit_bytes=VMEM_LIMIT),
        name="multiply",
    )(table, *operands)


def make_table(p_pattern, s_pattern, grid_col, layer, half, bases, zero_block):
    rows, groups, slots = p_pattern.shape
    mine = lax.dynamic_slice_in_dim(p_pattern, layer * half, half, 2)
    other = lax.dynamic_slice_in_dim(p_pattern, (1 - layer) * half, half, 2)
    inner = jnp.concatenate([mine, other], axis=2)
    targets = lax.dynamic_index_in_dim(mine, grid_col, 1, keepdims=False)
    total_rows = s_pattern.shape[0]
    ids = jnp.arange(total_rows, dtype=jnp.int32)
    hot = (inner.reshape(-1, 1) == ids[None, :]).astype(jnp.float32)
    lookup = jnp.concatenate([s_pattern[:, 0, :], bases[:, None]], axis=1).astype(jnp.float32)
    found = jnp.einsum("nk,kb->nb", hot, lookup, precision=lax.Precision.HIGHEST)
    found = found.astype(jnp.int32).reshape(rows, groups, slots, -1)
    s_rows, base = found[..., :-1], found[..., -1]
    match = (s_rows[:, :, None, :, :] == targets[:, None, :, None, None]) & (
        (targets >= 0)[:, None, :, None, None] & (inner >= 0)[:, :, None, :, None]
    )
    offset = jnp.arange(s_rows.shape[-1], dtype=jnp.int32)
    place = jnp.where(match, base[:, :, None, :, None] + offset - zero_block, 0)
    table = jnp.sum(place, axis=-1) + zero_block
    return jnp.transpose(table, (1, 0, 2, 3)).reshape(-1)


def per_device(p_blocks, s_blocks, p_pattern, s_pattern):
    rows, _, half, _, _ = p_blocks.shape
    slots = s_blocks.shape[2]
    n_row, n_col = lax.axis_size("row"), lax.axis_size("col")
    n_layer = lax.axis_size("depth")
    grid_row, grid_col = lax.axis_index("row"), lax.axis_index("col")
    layer = lax.axis_index("depth")
    row_half = rows // n_layer
    swap = [(0, 1), (1, 0)]

    def swap_where(keep):
        return [
            (z * n_layer + a, z * n_layer + b) for z in range(n_col) if keep(z) for a, b in swap
        ]

    p_mine = p_blocks[:, 0]
    cut = rows // CHUNKS
    spans = [(c * cut, rows if c == CHUNKS - 1 else (c + 1) * cut) for c in range(CHUNKS)]
    ups = [[p_mine[lo:hi]] for lo, hi in spans]
    downs = [[p_mine[lo:hi]] for lo, hi in spans]
    for s in range(1, n_col):
        up_pairs = [(i, i + 1) for i in range(s - 1, n_col - 1)]
        down_pairs = [(i, i - 1) for i in range(1, n_col - s + 1)]
        for c in range(CHUNKS):
            ups[c].append(lax.ppermute(ups[c][-1], "col", up_pairs))
            downs[c].append(lax.ppermute(downs[c][-1], "col", down_pairs))

    s_own = s_blocks[:, 0]
    s_half = lax.dynamic_slice_in_dim(s_own, layer * row_half, row_half, 0)
    below = (grid_row - 1) % n_row
    near_mine = lax.ppermute(s_half, "row", [(r, (r + 1) % n_row) for r in range(n_row)])
    far_mine = lax.ppermute(s_half, "row", [(r, (r - 1) % n_row) for r in range(n_row)])
    near_other = lax.ppermute(near_mine, "depth", swap)
    far_other = lax.ppermute(far_mine, "depth", swap)

    all_rows = jnp.arange(rows * n_row, dtype=jnp.int32)
    shard, local = all_rows // rows, all_rows % rows
    third = jnp.where(shard == below, 1, 2) * rows * slots
    halo = third + jnp.where(local // row_half == layer, 0, row_half * slots)
    bases = jnp.where(shard == grid_row, local * slots, halo + (local % row_half) * slots)
    total_groups = 3 * rows + 1
    zero_block = 3 * rows * slots
    table = make_table(p_pattern, s_pattern, grid_col, layer, half, bases, zero_block)
    table_size = table.shape[0]
    sources = jnp.array([0] + [w * s for s in range(1, n_col) for w in (-1, 1)], jnp.int32) + grid_col
    there = (sources >= 0) & (sources < n_col)
    pairs = jnp.stack([jnp.clip(sources, 0, n_col - 1), there.astype(jnp.int32)], axis=1)
    table = jnp.concatenate([table, pairs.reshape(-1)])

    s_split = prepare_own(table, s_own, total_groups)
    s_split = prepare_halo(s_split, near_mine, near_other, rows)
    s_split = prepare_halo(s_split, far_mine, far_other, 2 * rows)

    pending = [[] for _ in spans]
    for c in range(CHUNKS):
        p_other = lax.ppermute(ups[c][0], "depth", swap)
        pending[c].append((ups[c][0], p_other))
    result, first = None, 0
    for s in range(1, n_col):
        for c, (lo, hi) in enumerate(spans):
            up, down = ups[c][s], downs[c][s]
            up_other = lax.ppermute(up, ("col", "depth"), swap_where(lambda z: z >= s))
            down_other = lax.ppermute(down, ("col", "depth"), swap_where(lambda z: z + s < n_col))
            pending[c] += [(up, up_other), (down, down_other)]
        if s >= n_col - 2:
            for c, (lo, hi) in enumerate(spans):
                result = multiply(
                    table,
                    table_size + 2 * first,
                    pending[c],
                    s_split,
                    result,
                    rows,
                    lo,
                    first == 0,
                )
            first += len(pending[0])
            pending = [[] for _ in spans]
    return result[:, None]


def solution(mesh):
    in_specs = (
        P("row", "col", "depth", None, None),
        P("row", "col", None, None, None),
        P("row", None, None),
        P(None, "col", None),
    )
    out_specs = P("row", "col", "depth", None, None)

    return jax.shard_map(
        per_device, mesh=mesh, in_specs=in_specs, out_specs=out_specs, check_vma=False
    )
```
